512 devices in a mesh: tile: 128 (over z, y, core), lev: 4 (over x).
Axes of the slice: x: 4, y: 8, z: 8, core: 2. Of those that a mesh axis runs over, the one named last changes fastest.
Arguments:
- adj_out: bfloat16 [512, 8, 3, 128, 128], P('tile', 'lev'), may hold values from -6 to 6
- lat_weights: bfloat16 [8, 128, 128], replicated, may hold values from -0.5 to 0.5
- lon_weights: bfloat16 [8, 128, 128], replicated, may hold values from -0.5 to 0.5
- counts: int32 [512], P('tile'), may hold values from 2 to 12, as said below
- departures: int32 [512, 12], P('tile'), may hold values from 0 to 511, as said below
- blocks: int32 [512, 12, 2], P('tile'), may hold values from 0 to 7
- upper_coef: bfloat16 [512, 8, 128, 128], P('tile', 'lev'), may hold values from 0.19921875 to 1
- lower_coef: bfloat16 [512, 8, 128, 128], P('tile', 'lev'), may hold values from 0.19921875 to 1
Outputs:
- adj_in: bfloat16 [512, 8, 3, 128, 128], P('tile', 'lev')
The draws below stay inside these ranges and needn't reach their ends.
Inputs may be any that keep to these rules, and one draw needn't show every extreme that they name: `counts`: every tile has 2 to 12 live slots; some tiles have exactly 12. The 4 tiles of one index of tile hold at most 27 live slots together, and some index of tile holds exactly 27. `departures`: every slot's source tile, live or not, belongs to an index of tile at most 2 places away from the index that holds the slot's tile, counted around the tile axis with wrap-around.
All inputs are finite; a program needn't handle non-finite values.
Results may differ from the reference program's by a relative error of at most 0.0062.
Values may be sent and summed in bfloat16 or wider, within the bound.
No kernel may reach another device: no remote copies, remote signals or barrier semaphores. Data moves between devices by JAX's collectives and lax.ppermute only.
A program may use at most 128 MiB of HBM per device.

```python
import jax
import jax.numpy as jnp
from jax import lax

S = 128
FIELDS = 3
TPD = 4
KMAX = 12
KCALM = 5
REACH = 2
NB = 8
TILES = 512
LEV = 8
N_TILE = 128


def draw_counts(key, part):
    device_total = TILES // TPD
    subkeys = jax.random.split(key, 4)
    drawn_counts = jax.random.randint(subkeys[0], (device_total, TPD), 2, KCALM + 1)
    jet_start = jax.random.randint(subkeys[1], (), 0, device_total)
    jet_span = max(device_total // 4, 1)
    device_pos = jnp.arange(device_total)
    jet_device = (device_pos - jet_start) % device_total < jet_span
    full_device = jax.random.randint(subkeys[2], (), 0, device_total)
    jet_device = jet_device | (device_pos == full_device)
    jet_tile = jax.random.randint(subkeys[3], (device_total,), 0, TPD)
    drawn_counts = jnp.where((device_pos == full_device)[:, None], KCALM, drawn_counts)
    is_jet = jet_device[:, None] & (jnp.arange(TPD)[None, :] == jet_tile[:, None])
    return jnp.where(is_jet, KMAX, drawn_counts).reshape(TILES).astype(jnp.int32)


def draw_departures(key, part):
    device_total = TILES // TPD
    subkeys = jax.random.split(key, 2)
    tile_device = jnp.arange(TILES) // TPD
    offsets = jax.random.randint(subkeys[0], (TILES, KMAX), -REACH, REACH + 1)
    within = jax.random.randint(subkeys[1], (TILES, KMAX), 0, TPD)
    return ((tile_device[:, None] + offsets) % device_total * TPD + within).astype(jnp.int32)


def plant(array, own_key, least, high):
    shape = array.shape
    index_at = [jax.random.randint(jax.random.fold_in(own_key, axis), (), 0, shape[axis]) for axis in range(len(shape))]
    array = array.at[tuple(index_at)].set(least)
    longest = shape.index(max(shape))
    index_at[longest] = (index_at[longest] + 1) % shape[longest]
    return array.at[tuple(index_at)].set(high)


def block_scale(key, dims, shards, smallest, largest):
    def one(axis_at, parts):
        steps = jax.random.uniform(jax.random.fold_in(jax.random.fold_in(key, 6), axis_at), (parts,), jnp.float32, smallest / len(shards), largest / len(shards))
        return jnp.repeat(jnp.exp(steps), dims[axis_at] // parts).reshape((-1,) + (1,) * (len(dims) - axis_at - 1))

    factor_of = one(*shards[0])
    for cut in shards[1:]:
        factor_of = factor_of * one(*cut)
    return factor_of


def noise(key, shape, scale, most, pieces=(), held_as=jnp.bfloat16):
    result = scale * jax.random.normal(key, shape, jnp.float32)
    if pieces:
        result = result * block_scale(key, shape, pieces, -0.22, 0.18)
    return jnp.clip(result, -most, most).astype(held_as)


def setup_inputs(seed: int = 0) -> dict:
    streams_of = jax.random.split(jax.random.key(seed), 9)
    return {
        "adj_out": noise(streams_of[0], (TILES, LEV, FIELDS, S, S), 1.0, 6.0, ((0, 128), (1, 4))),
        "lat_weights": noise(streams_of[1], (NB, S, S), S ** -0.5, 0.5),
        "lon_weights": noise(streams_of[2], (NB, S, S), S ** -0.5, 0.5),
        "counts": draw_counts(jax.random.fold_in(streams_of[8], 71), 0),
        "departures": draw_departures(jax.random.fold_in(streams_of[8], 71), 0),
        "blocks": plant(jax.random.randint(streams_of[5], (TILES, KMAX, 2), 0, NB), jax.random.fold_in(streams_of[5], 1), 0, NB - 1).astype(jnp.int32),
        "upper_coef": jnp.clip(0.19921875 + 0.80078125 * jax.random.uniform(streams_of[6], (TILES, LEV, S, S), jnp.float32) ** block_scale(streams_of[6], (TILES, LEV, S, S), ((0, 128), (1, 4)), -0.2, 0.2), 0.19921875, 1.0).astype(jnp.bfloat16),
        "lower_coef": jnp.clip(0.19921875 + 0.80078125 * jax.random.uniform(streams_of[7], (TILES, LEV, S, S), jnp.float32) ** block_scale(streams_of[7], (TILES, LEV, S, S), ((0, 128), (1, 4)), -0.2, 0.2), 0.19921875, 1.0).astype(jnp.bfloat16),
    }


def group_bundle(adj_out, lat_weights, lon_weights, counts, departures, blocks, group_index):
    first_tile = group_index * TPD
    cotangent = lax.dynamic_slice_in_dim(adj_out, first_tile, TPD, 0).astype(jnp.float32)
    tile_counts = lax.dynamic_slice_in_dim(counts, first_tile, TPD, 0)
    sources = lax.dynamic_slice_in_dim(departures, first_tile, TPD, 0)
    chosen = lax.dynamic_slice_in_dim(blocks, first_tile, TPD, 0)
    live_mask = (jnp.arange(KMAX, dtype=jnp.int32)[None, :] < tile_counts[:, None]).astype(jnp.float32)
    lat_sel = jnp.take(lat_weights, chosen[:, :, 0], axis=0).astype(jnp.float32)
    lon_sel = jnp.take(lon_weights, chosen[:, :, 1], axis=0).astype(jnp.float32)
    lat_applied = jnp.einsum('tkab,tlfac->tklfbc', lat_sel, cotangent, precision=lax.Precision.HIGHEST).astype(jnp.bfloat16)
    slot_part = jnp.einsum('tklfbc,tkcd->tklfbd', lat_applied.astype(jnp.float32), lon_sel, precision=lax.Precision.HIGHEST).astype(jnp.bfloat16)
    window = (2 * REACH + 1) * TPD
    base_tile = ((group_index - REACH) % N_TILE) * TPD
    local_rows = (sources - base_tile) % TILES
    select = (local_rows[:, :, None] == jnp.arange(window, dtype=jnp.int32)[None, None, :]).astype(jnp.float32) * live_mask[:, :, None]
    bundle = jnp.einsum('tkw,tklfbd->wlfbd', select, slot_part.astype(jnp.float32), precision=lax.Precision.HIGHEST).astype(jnp.bfloat16)
    return bundle, base_tile


def reference(adj_out, lat_weights, lon_weights, counts, departures, blocks, upper_coef, lower_coef):
    window = (2 * REACH + 1) * TPD
    accumulated = jnp.zeros(adj_out.shape, jnp.float32)

    def add_group(carried, group_index):
        bundle, base_tile = group_bundle(adj_out, lat_weights, lon_weights, counts, departures, blocks, group_index)
        target_rows = (base_tile + jnp.arange(window, dtype=jnp.int32)) % TILES
        return carried.at[target_rows].add(bundle.astype(jnp.float32)), None

    interp, _ = lax.scan(add_group, accumulated, jnp.arange(N_TILE, dtype=jnp.int32))
    upper_rate = upper_coef.astype(jnp.float32)[:, :, None]
    lower_rate = lower_coef.astype(jnp.float32)[:, :, None]
    upflow = upper_rate * interp
    downflow = lower_rate * interp
    from_lower = jnp.concatenate([jnp.zeros_like(upflow[:, :1]), upflow[:, :-1]], axis=1)
    from_upper = jnp.concatenate([downflow[:, 1:], jnp.zeros_like(downflow[:, :1])], axis=1)
    return ((1.0 + upper_rate + lower_rate) * interp - from_lower - from_upper).astype(jnp.bfloat16)
```

```python
import jax
import jax.numpy as jnp
from jax import lax
from jax.experimental import pallas as pl
from jax.experimental.pallas import tpu as pltpu
from jax.sharding import PartitionSpec as P

REACH = 2
DEAD = 64
VMEM = pl.BlockSpec(memory_space=pltpu.VMEM)
SMEM = pl.BlockSpec(memory_space=pltpu.SMEM)


def gather_slots(meta_ref, where, tiles, slots, first, code_list, block_list, base):
    n = base
    for t in range(tiles):
        for k in range(slots):
            i = t * slots + k
            s = meta_ref[0, i] - first
            hit = jnp.logical_and(s >= 0, s < tiles)
            code_list[n] = s * (2 * tiles) + (where * tiles + t)
            block_list[n] = meta_ref[1, i]
            n = n + hit.astype(jnp.int32)
    return n


def add_slots(n, source_refs, tiles, planes, size, code_list, block_list, lat_t_ref, lon_ref, acc_ref):
    rows = planes * size
    code_list[n] = tiles * (2 * tiles)
    block_list[n] = 0

    def one(i):
        code = code_list[i]
        blk = block_list[i]
        s = code // (2 * tiles)
        t = code % (2 * tiles)
        lat_t = lat_t_ref[blk // 8]
        lon = lon_ref[blk % 8]
        return s, t, lat_t, lon

    def part(ref, t, lat_t):
        a = ref[pl.ds(pl.multiple_of(t * rows, rows), rows), :]
        outs = []
        for j in range(0, planes, 2):
            pair = jnp.concatenate(
                [a[j * size : (j + 1) * size], a[(j + 1) * size : (j + 2) * size]], axis=1
            )
            p = jnp.dot(lat_t, pair, preferred_element_type=jnp.float32).astype(jnp.bfloat16)
            outs += [p[:, :size], p[:, size:]]
        return jnp.concatenate(outs, axis=0)

    (ref,) = source_refs

    def body(i, carry):
        s0, t0, lt0, ln0 = one(2 * i)
        s1, t1, lt1, ln1 = one(2 * i + 1)
        p0 = part(ref, t0, lt0)
        p1 = part(ref, t1, lt1)
        q0 = jnp.dot(p0, ln0, preferred_element_type=jnp.float32)
        q1 = jnp.dot(p1, ln1, preferred_element_type=jnp.float32)
        acc_ref[s0] += q0
        acc_ref[s1] += q1
        return carry

    lax.fori_loop(0, (n + 1) // 2, body, 0)


def phase(source, meta, shift, lat_t, lon, acc, tiles, slots, planes, size):
    def kernel(*refs):
        if acc is None:
            shift_ref, meta_ref, src, lat_ref, lon_ref, out_ref, code_list, block_list = refs
            out_ref[...] = jnp.zeros_like(out_ref)
        else:
            shift_ref, meta_ref, src, lat_ref, lon_ref, acc_ref, out_ref, code_list, block_list = refs
        n = gather_slots(meta_ref, 0, tiles, slots, shift_ref[0], code_list, block_list, 0)
        add_slots(n, (src,), tiles, planes, size, code_list, block_list, lat_ref, lon_ref, out_ref)

    args = [shift, meta, source, lat_t, lon]
    specs = [SMEM, SMEM, VMEM, VMEM, VMEM]
    if acc is not None:
        args.append(acc)
        specs.append(VMEM)
    return pl.pallas_call(
        kernel,
        out_shape=jax.ShapeDtypeStruct((tiles + 1, planes * size, size), jnp.float32),
        in_specs=specs,
        out_specs=VMEM,
        scratch_shapes=[
            pltpu.SMEM((tiles * slots + 2,), jnp.int32),
            pltpu.SMEM((tiles * slots + 2,), jnp.int32),
        ],
        input_output_aliases={} if acc is None else {5: 0},
        compiler_params=pltpu.CompilerParams(vmem_limit_bytes=40 << 20),
    )(*args)


def flows(acc, upper, lower, tiles, levels, fields, size):
    def kernel(acc_ref, upper_ref, lower_ref, up_ref, down_ref):
        for s in range(tiles):
            u = upper_ref[s, levels - 1].astype(jnp.float32)
            d = lower_ref[s, 0].astype(jnp.float32)
            for f in range(fields):
                top = ((levels - 1) * fields + f) * size
                up_ref[s, f] = (u * acc_ref[s, top : top + size]).astype(jnp.bfloat16)
                down_ref[s, f] = (d * acc_ref[s, f * size : (f + 1) * size]).astype(jnp.bfloat16)

    rim = jax.ShapeDtypeStruct((tiles, fields, size, size), jnp.bfloat16)
    return pl.pallas_call(
        kernel,
        out_shape=(rim, rim),
        in_specs=[VMEM] * 3,
        out_specs=(VMEM, VMEM),
        compiler_params=pltpu.CompilerParams(vmem_limit_bytes=40 << 20),
    )(acc, upper, lower)


def couple(acc, upper, lower, rim_low, rim_up, tiles, levels, fields, size):
    def kernel(acc_ref, upper_ref, lower_ref, low_ref, up_ref, out_ref):
        us = [upper_ref[0, l].astype(jnp.float32) for l in range(levels)]
        ds = [lower_ref[0, l].astype(jnp.float32) for l in range(levels)]
        for f in range(fields):
            v = [acc_ref[0, (l * fields + f) * size : (l * fields + f + 1) * size] for l in range(levels)]
            for l in range(levels):
                below = low_ref[0, f].astype(jnp.float32) if l == 0 else us[l - 1] * v[l - 1]
                above = up_ref[0, f].astype(jnp.float32) if l == levels - 1 else ds[l + 1] * v[l + 1]
                out_ref[0, l, f] = ((1.0 + us[l] + ds[l]) * v[l] - below - above).astype(jnp.bfloat16)

    coef = pl.BlockSpec((1, levels, size, size), lambda s: (s, 0, 0, 0))
    rim = pl.BlockSpec((1, fields, size, size), lambda s: (s, 0, 0, 0))
    return pl.pallas_call(
        kernel,
        grid=(tiles,),
        out_shape=jax.ShapeDtypeStruct((tiles, levels, fields, size, size), jnp.bfloat16),
        in_specs=[
            pl.BlockSpec((1, levels * fields * size, size), lambda s: (s, 0, 0)),
            coef,
            coef,
            rim,
            rim,
        ],
        out_specs=pl.BlockSpec((1, levels, fields, size, size), lambda s: (s, 0, 0, 0, 0)),
        compiler_params=pltpu.CompilerParams(vmem_limit_bytes=40 << 20),
    )(acc, upper, lower, rim_low, rim_up)


def passed_along(x, axis, by):
    length = lax.axis_size(axis)
    pairs = [(i, i + by) for i in range(length) if 0 <= i + by < length]
    return lax.ppermute(x, axis, pairs)


def per_device(
    adj_out, lat_weights, lon_weights, counts, departures, blocks, upper_coef, lower_coef
):
    tile_devices = lax.axis_size("tile")
    own_index = lax.axis_index("tile")
    tiles, slots = departures.shape
    levels, fields, size = adj_out.shape[1], adj_out.shape[2], adj_out.shape[3]
    planes = levels * fields
    rows = tiles * planes * size
    base_tile = (own_index - REACH) % tile_devices * tiles
    window_row = (departures - base_tile) % (tile_devices * tiles)
    live = jnp.arange(slots, dtype=jnp.int32)[None, :] < counts[:, None]
    meta = jnp.stack(
        [
            jnp.where(live, window_row, DEAD).reshape(-1),
            (blocks[:, :, 0] * 8 + blocks[:, :, 1]).reshape(-1),
        ]
    )
    flat = adj_out.reshape(rows, size)
    tail = jnp.pad(meta.astype(jnp.bfloat16), ((0, 14), (0, size - tiles * slots)))
    packed = jnp.concatenate([flat, tail], axis=0)

    def unpack_meta(arrived):
        return arrived[rows : rows + 2, : tiles * slots].astype(jnp.int32)

    def permuted(x, even_by, odd_by):
        pairs = [(i, (i + (even_by if i % 2 == 0 else odd_by)) % tile_devices) for i in range(tile_devices)]
        return lax.ppermute(x, "tile", pairs)

    odd = own_index % 2
    sign = 1 - 2 * odd

    def shift(offset):
        return ((REACH - offset) * tiles).reshape(1).astype(jnp.int32)

    lat_t = jnp.swapaxes(lat_weights, 1, 2)
    x_in = permuted(packed, -2, 2)
    mate = permuted(packed, 1, -1)

    def step(source, source_meta, offset, acc):
        return phase(source, source_meta, shift(offset), lat_t, lon_weights, acc, tiles, slots, planes, size)

    acc = step(flat, meta, 0 * sign, None)
    packed_y, acc = lax.optimization_barrier((packed, acc))
    y_in = permuted(packed_y, 2, -2)
    acc = step(mate, unpack_meta(mate), sign, acc)
    x_mate = permuted(x_in, 1, -1)
    acc = step(x_in, unpack_meta(x_in), 2 * sign, acc)
    acc = step(x_mate, unpack_meta(x_mate), -sign, acc)
    acc = step(y_in, unpack_meta(y_in), -2 * sign, acc)
    up, down = flows(acc, upper_coef, lower_coef, tiles, levels, fields, size)
    rim_low = passed_along(up, "lev", 1)
    rim_up = passed_along(down, "lev", -1)
    return couple(acc, upper_coef, lower_coef, rim_low, rim_up, tiles, levels, fields, size)


def solution(mesh):
    placed = (
        P("tile", "lev", None, None, None),
        P(),
        P(),
        P("tile"),
        P("tile", None),
        P("tile", None, None),
        P("tile", "lev", None, None),
        P("tile", "lev", None, None),
    )
    return jax.shard_map(
        per_device,
        mesh=mesh,
        in_specs=placed,
        out_specs=P("tile", "lev", None, None, None),
        check_vma=False,
    )
```

```python
import jax
import jax.numpy as jnp
from jax import lax
from jax.experimental import pallas as pl
from jax.experimental.pallas import tpu as pltpu
from jax.sharding import PartitionSpec as P

REACH = 2
DEAD = 64
META = 16
O_FLOPS = 1 << 0
M_FLOPS = 1 << 36
XM_FLOPS = 1 << 0
L_FLOPS = 1 << 0
VMEM = pl.BlockSpec(memory_space=pltpu.VMEM)
SMEM = pl.BlockSpec(memory_space=pltpu.SMEM)
HBM = pl.BlockSpec(memory_space=pltpu.HBM)
COST = pl.CostEstimate(flops=1, transcendentals=0, bytes_accessed=1)
PARAMS = pltpu.CompilerParams(vmem_limit_bytes=6 << 20)


def in_hbm(x):
    return pltpu.with_memory_space_constraint(x, pltpu.HBM)


def pack(flat, counts, departures, blocks, base):
    rows, size = flat.shape
    tiles, slots = departures.shape
    wrap = lax.axis_size("tile") * tiles

    def kernel(base_ref, counts_hbm, dep_hbm, blk_hbm, flat_hbm, out_hbm, counts_ref, dep, blk, meta, tail, body, sems):
        copies = [
            pltpu.make_async_copy(counts_hbm, counts_ref, sems.at[0]),
            pltpu.make_async_copy(dep_hbm, dep, sems.at[1]),
            pltpu.make_async_copy(blk_hbm, blk, sems.at[2]),
            pltpu.make_async_copy(flat_hbm, body, sems.at[3]),
        ]
        for c in copies:
            c.start()
        meta[...] = jnp.zeros_like(meta)
        for c in copies[:3]:
            c.wait()
        w = dep[...] - base_ref[0]
        w = jnp.where(w < 0, w + wrap, w)
        k = lax.broadcasted_iota(jnp.int32, (1, slots), 1)
        for t in range(tiles):
            at = slice(t * slots, (t + 1) * slots)
            meta[0:1, at] = jnp.where(k < counts_ref[t], w[t : t + 1], DEAD).astype(jnp.float32)
            meta[1:2, at] = (blk[t, 0:1] * 8 + blk[t, 1:2]).astype(jnp.float32)
        tail[...] = meta[...].astype(jnp.bfloat16)
        last = pltpu.make_async_copy(tail, out_hbm.at[pl.ds(rows, META)], sems.at[4])
        last.start()
        copies[3].wait()
        out = pltpu.make_async_copy(body, out_hbm.at[pl.ds(0, rows)], sems.at[5])
        out.start()
        last.wait()
        out.wait()

    return pl.pallas_call(
        kernel,
        out_shape=pltpu.HBM((rows + META, size), flat.dtype),
        in_specs=[SMEM, HBM, HBM, HBM, HBM],
        out_specs=HBM,
        scratch_shapes=[
            pltpu.SMEM((tiles,), jnp.int32),
            pltpu.VMEM((tiles, slots), jnp.int32),
            pltpu.VMEM((tiles, 2, slots), jnp.int32),
            pltpu.VMEM((META, size), jnp.float32),
            pltpu.VMEM((META, size), jnp.bfloat16),
            pltpu.VMEM((rows, size), jnp.bfloat16),
            pltpu.SemaphoreType.DMA((6,)),
        ],
        compiler_params=PARAMS,
        cost_estimate=COST,
    )(base, in_hbm(counts), in_hbm(departures), in_hbm(blocks), in_hbm(flat))


def append_slots(shift, tiles, slots, where, meta_s, entries, n):
    for t in range(tiles):
        for k in range(slots):
            code = meta_s[0, t * slots + k]
            s = (code >> 6) - shift
            entries[n] = (s << 16) | ((code & 63) << 8) | (where * tiles + t)
            n = n + jnp.logical_and(s >= 0, s < tiles).astype(jnp.int32)
    return n


def add_slots(n, load, planes, size, entries, table_ref, acc_ref):
    blocks = table_ref.shape[0] // 2
    def half(i):
        entry = entries[i]
        a = load(entry & 255)
        lat_t = table_ref[(entry >> 11) & 7]
        outs = []
        for j in range(0, planes, 2):
            pair = jnp.concatenate([a[j * size : (j + 1) * size], a[(j + 1) * size : (j + 2) * size]], axis=1)
            p = jnp.dot(lat_t, pair, preferred_element_type=jnp.float32).astype(jnp.bfloat16)
            outs += [p[:, :size], p[:, size:]]
        return entry >> 16, (entry >> 8) & 7, jnp.concatenate(outs, axis=0)

    def body(i, carry):
        s0, b0, p0 = half(2 * i)
        s1, b1, p1 = half(2 * i + 1)
        q0 = jnp.dot(p0, table_ref[blocks + b0], preferred_element_type=jnp.float32)
        q1 = jnp.dot(p1, table_ref[blocks + b1], preferred_element_type=jnp.float32)
        acc_ref[s0] += q0
        acc_ref[s1] += q1
        return carry

    lax.fori_loop(0, (n + 1) >> 1, body, 0)


def ready_tables(lat, lon, later_than):
    blocks = lat.shape[0]

    def kernel(lat_hbm, lon_hbm, _, out_ref, held, sems):
        copies = [
            pltpu.make_async_copy(lat_hbm, held, sems.at[0]),
            pltpu.make_async_copy(lon_hbm, out_ref.at[pl.ds(blocks, blocks)], sems.at[1]),
        ]
        for c in copies:
            c.start()
        copies[0].wait()
        for b in range(blocks):
            out_ref[b] = held[b].T
        copies[1].wait()

    return pl.pallas_call(
        kernel,
        out_shape=jax.ShapeDtypeStruct((2 * blocks,) + lat.shape[1:], lat.dtype),
        in_specs=[HBM] * 3,
        out_specs=VMEM,
        scratch_shapes=[pltpu.VMEM(lat.shape, lat.dtype), pltpu.SemaphoreType.DMA((2,))],
        compiler_params=PARAMS,
        cost_estimate=COST,
    )(in_hbm(lat), in_hbm(lon), later_than)


def phase(sources, sign, offsets, tables, acc, coefs, tiles, slots, levels, fields, size, flops=1):
    planes = levels * fields
    rows = planes * size
    data = tiles * rows
    last = coefs is not None
    fresh = acc is None
    count = len(sources)

    def kernel(sign_ref, *refs):
        srcs, refs = refs[:count], refs[count:]
        refs = refs[1 if fresh else 2 :]
        if last:
            upper_hbm, lower_hbm, table_ref, acc_ref, up_ref, down_ref, upper_ref, lower_ref = refs[:8]
        else:
            table_ref, acc_ref = refs[:2]
        src, tail, meta_v, meta_s, entries, sems = refs[-6:]
        tails = [pltpu.make_async_copy(srcs[g].at[pl.ds(data, META)], tail.at[g], sems.at[g]) for g in range(count)]
        metas = [pltpu.make_async_copy(meta_v.at[g], meta_s.at[g], sems.at[g]) for g in range(count)]
        datas = [
            pltpu.make_async_copy(srcs[g].at[pl.ds(0, data)], src.at[pl.ds(g * data, data)], sems.at[count + g])
            for g in range(count)
        ]
        late = []
        if last:
            late = [
                pltpu.make_async_copy(upper_hbm, upper_ref, sems.at[2 * count]),
                pltpu.make_async_copy(lower_hbm, lower_ref, sems.at[2 * count + 1]),
            ]
        for c in tails + datas + late:
            c.start()
        if fresh:
            acc_ref[...] = jnp.zeros_like(acc_ref)
        for g in range(count):
            tails[g].wait()
            slot_data = tail[g].astype(jnp.float32)
            meta_v[g] = (slot_data[0:1] * 64.0 + slot_data[1:2]).astype(jnp.int32)
            metas[g].start()
        n = 0
        for g in range(count):
            metas[g].wait()
            n = append_slots((REACH - offsets[g] * sign_ref[0]) * tiles, tiles, slots, g, meta_s.at[g], entries, n)
        entries[n] = tiles << 16
        for c in datas:
            c.wait()

        def load(t):
            return src[pl.ds(pl.multiple_of(t * rows, rows), rows), :]

        add_slots(n, load, planes, size, entries, table_ref, acc_ref)
        if not last:
            return
        for c in late:
            c.wait()
        for s in range(tiles):
            u = upper_ref[s, levels - 1].astype(jnp.float32)
            d = lower_ref[s, 0].astype(jnp.float32)
            for f in range(fields):
                top = ((levels - 1) * fields + f) * size
                up_ref[s, f] = (u * acc_ref[s, top : top + size]).astype(jnp.bfloat16)
                down_ref[s, f] = (d * acc_ref[s, f * size : (f + 1) * size]).astype(jnp.bfloat16)

    args = [sign, *sources, tables]
    specs = [SMEM] + [HBM] * count + [VMEM]
    if not fresh:
        args.append(acc)
        specs.append(VMEM)
    out_shape = [jax.ShapeDtypeStruct(tables.shape, tables.dtype), jax.ShapeDtypeStruct((tiles + 1, rows, size), jnp.float32)]
    if last:
        args += [in_hbm(c) for c in coefs]
        specs += [HBM, HBM]
        out_shape += [jax.ShapeDtypeStruct((tiles, fields, size, size), jnp.bfloat16)] * 2
        out_shape += [jax.ShapeDtypeStruct(c.shape, c.dtype) for c in coefs]
    return pl.pallas_call(
        kernel,
        out_shape=out_shape,
        in_specs=specs,
        out_specs=[VMEM] * len(out_shape),
        scratch_shapes=[
            pltpu.VMEM((count * data, size), jnp.bfloat16),
            pltpu.VMEM((count, META, size), jnp.bfloat16),
            pltpu.VMEM((count, 1, size), jnp.int32),
            pltpu.SMEM((count, 1, size), jnp.int32),
            pltpu.SMEM((count * tiles * slots + 2,), jnp.int32),
            pltpu.SemaphoreType.DMA((2 * count + 2,)),
        ],
        input_output_aliases={count + 1: 0} if fresh else {count + 1: 0, count + 2: 1},
        compiler_params=PARAMS,
        cost_estimate=pl.CostEstimate(flops=flops, transcendentals=0, bytes_accessed=1),
    )(*args)


def couple(out, sums, upper, lower, rim_low, rim_up, tiles, levels, fields, size, first, last):
    own = last - first

    def kernel(sum_ref, upper_ref, lower_ref, low_ref, up_ref, *refs):
        out_ref, buf, sems = refs[-3:]
        copies = []
        for s in range(tiles):
            us = [upper_ref[s, l].astype(jnp.float32) for l in range(levels)]
            ds = [lower_ref[s, l].astype(jnp.float32) for l in range(levels)]
            for f in range(own):
                v = [sum_ref[s, (l * own + f) * size : (l * own + f + 1) * size] for l in range(levels)]
                for l in range(levels):
                    below = low_ref[s, f].astype(jnp.float32) if l == 0 else us[l - 1] * v[l - 1]
                    above = up_ref[s, f].astype(jnp.float32) if l == levels - 1 else ds[l + 1] * v[l + 1]
                    buf[s, l, f] = ((1.0 + us[l] + ds[l]) * v[l] - below - above).astype(jnp.bfloat16)
            c = pltpu.make_async_copy(buf.at[s], out_ref.at[s, :, pl.ds(first, own)], sems.at[s])
            c.start()
            copies.append(c)
        for c in copies:
            c.wait()

    args = [sums, upper, lower, rim_low, rim_up]
    specs = [VMEM] * 5
    if out is not None:
        args.append(out)
        specs.append(HBM)
    return pl.pallas_call(
        kernel,
        out_shape=jax.ShapeDtypeStruct((tiles, levels, fields, size, size), jnp.bfloat16),
        in_specs=specs,
        out_specs=HBM,
        scratch_shapes=[
            pltpu.VMEM((tiles, levels, own, size, size), jnp.bfloat16),
            pltpu.SemaphoreType.DMA((tiles,)),
        ],
        input_output_aliases={} if out is None else {5: 0},
        compiler_params=PARAMS,
        cost_estimate=COST,
    )(*args)


def passed_along(x, axis, by):
    length = lax.axis_size(axis)
    pairs = [(i, i + by) for i in range(length) if 0 <= i + by < length]
    return lax.ppermute(x, axis, pairs)


def per_device(
    adj_out, lat_weights, lon_weights, counts, departures, blocks, upper_coef, lower_coef
):
    tile_devices = lax.axis_size("tile")
    own_index = lax.axis_index("tile")
    tiles, slots = departures.shape
    levels, fields, size = adj_out.shape[1], adj_out.shape[2], adj_out.shape[3]
    planes = levels * fields
    rows = tiles * planes * size
    base_tile = ((own_index - REACH) % tile_devices * tiles).reshape(1)
    packed = pack(adj_out.reshape(rows, size), counts, departures, jnp.swapaxes(blocks, 1, 2), base_tile)

    def permuted(x, even_by, odd_by):
        pairs = [(i, (i + (even_by if i % 2 == 0 else odd_by)) % tile_devices) for i in range(tile_devices)]
        return lax.ppermute(x, "tile", pairs)

    sign = 1 - 2 * (own_index % 2)

    sign = sign.reshape(1).astype(jnp.int32)
    sizes = tiles, slots, levels, fields, size
    x_in = permuted(packed, -2, 2)
    later, tables = lax.optimization_barrier((packed, ready_tables(lat_weights, lon_weights, packed)))
    mate = permuted(later, 1, -1)
    y_in = permuted(later, 2, -2)
    tables, acc = phase((packed,), sign, (0,), tables, None, None, *sizes, O_FLOPS)
    x_in, acc = lax.optimization_barrier((x_in, acc))
    x_mate = permuted(x_in, 1, -1)
    tables, acc = phase((x_in, mate), sign, (2, 1), tables, acc, None, *sizes, M_FLOPS)
    x_mate, acc = lax.optimization_barrier((x_mate, acc))
    tables, acc = phase((x_mate,), sign, (-1,), tables, acc, None, *sizes, XM_FLOPS)
    y_in, acc = lax.optimization_barrier((y_in, acc))
    _, acc, up, down, upper, lower = phase((y_in,), sign, (-2,), tables, acc, (upper_coef, lower_coef), *sizes, L_FLOPS)
    rim_low = passed_along(up, "lev", 1)
    rim_up = passed_along(down, "lev", -1)
    return couple(None, acc, upper, lower, rim_low, rim_up, tiles, levels, fields, size, 0, fields)


def solution(mesh):
    placed = (
        P("tile", "lev", None, None, None),
        P(),
        P(),
        P("tile"),
        P("tile", None),
        P("tile", None, None),
        P("tile", "lev", None, None),
        P("tile", "lev", None, None),
    )
    return jax.shard_map(
        per_device,
        mesh=mesh,
        in_specs=placed,
        out_specs=P("tile", "lev", None, None, None),
        check_vma=False,
    )
```

```python
import jax
import jax.numpy as jnp
from jax import lax
from jax.experimental import pallas as pl
from jax.experimental.pallas import tpu as pltpu
from jax.sharding import PartitionSpec as P

REACH = 2
DEAD = 64
META = 16
O_FLOPS = 1 << 0
M_FLOPS = 1 << 36
XM_FLOPS = 1 << 0
L_FLOPS = 1 << 0
T_FLOPS = 1 << 36
VMEM = pl.BlockSpec(memory_space=pltpu.VMEM)
SMEM = pl.BlockSpec(memory_space=pltpu.SMEM)
HBM = pl.BlockSpec(memory_space=pltpu.HBM)
COST = pl.CostEstimate(flops=1, transcendentals=0, bytes_accessed=1)
PARAMS = pltpu.CompilerParams(vmem_limit_bytes=6 << 20)


def in_hbm(x):
    return pltpu.with_memory_space_constraint(x, pltpu.HBM)


def pack(adj_out, counts, departures, blocks, base):
    tiles, levels, fields, size, _ = adj_out.shape
    rows = fields * size
    slots = departures.shape[1]
    wrap = lax.axis_size("tile") * tiles
    flat = adj_out.reshape(tiles, levels, rows, size)

    def kernel(base_ref, counts_hbm, dep_hbm, blk_hbm, flat_hbm, out_ref, counts_ref, dep, blk, meta, sems):
        copies = [
            pltpu.make_async_copy(counts_hbm, counts_ref, sems.at[0]),
            pltpu.make_async_copy(dep_hbm, dep, sems.at[1]),
            pltpu.make_async_copy(blk_hbm, blk, sems.at[2]),
        ]
        for l in range(levels):
            for t in range(tiles):
                at = (l * tiles + t) * rows + (META if l else 0)
                copies.append(
                    pltpu.make_async_copy(flat_hbm.at[t, l], out_ref.at[pl.ds(at, rows)], sems.at[3 + l * tiles + t])
                )
        for c in copies:
            c.start()
        meta[...] = jnp.zeros_like(meta)
        for c in copies[:3]:
            c.wait()
        w = dep[...] - base_ref[0]
        w = jnp.where(w < 0, w + wrap, w)
        k = lax.broadcasted_iota(jnp.int32, (1, slots), 1)
        for t in range(tiles):
            at = slice(t * slots, (t + 1) * slots)
            meta[0:1, at] = jnp.where(k < counts_ref[t], w[t : t + 1], DEAD).astype(jnp.float32)
            meta[1:2, at] = (blk[t, 0:1] * 8 + blk[t, 1:2]).astype(jnp.float32)
        out_ref[tiles * rows : tiles * rows + META, :] = meta[...].astype(jnp.bfloat16)
        for c in copies[3:]:
            c.wait()

    return pl.pallas_call(
        kernel,
        out_shape=jax.ShapeDtypeStruct((tiles * levels * rows + META, size), adj_out.dtype),
        in_specs=[SMEM, HBM, HBM, HBM, HBM],
        out_specs=VMEM,
        scratch_shapes=[
            pltpu.SMEM((tiles,), jnp.int32),
            pltpu.VMEM((tiles, slots), jnp.int32),
            pltpu.VMEM((tiles, 2, slots), jnp.int32),
            pltpu.VMEM((META, size), jnp.float32),
            pltpu.SemaphoreType.DMA((3 + tiles * levels,)),
        ],
        compiler_params=PARAMS,
        cost_estimate=COST,
    )(base, in_hbm(counts), in_hbm(departures), in_hbm(blocks), in_hbm(flat))


def append_slots(shift, tiles, slots, where, meta_s, entries, n):
    for t in range(tiles):
        for k in range(slots):
            code = meta_s[0, t * slots + k]
            s = (code >> 6) - shift
            entries[n] = (s << 16) | ((code & 63) << 8) | (where * tiles + t)
            n = n + jnp.logical_and(s >= 0, s < tiles).astype(jnp.int32)
    return n


def add_slots(n, load, planes, size, first, entries, table_ref, acc_ref):
    blocks = table_ref.shape[0] // 2
    rows = planes * size

    def half(i):
        entry = entries[i]
        a = load(entry & 255)
        lat_t = table_ref[(entry >> 11) & 7]
        outs = []
        for j in range(0, planes, 2):
            if j + 1 == planes:
                wide = a[j]
            else:
                wide = jnp.concatenate([a[j], a[j + 1]], axis=1)
            p = jnp.dot(lat_t, wide, preferred_element_type=jnp.float32).astype(jnp.bfloat16)
            outs += [p] if j + 1 == planes else [p[:, :size], p[:, size:]]
        return entry >> 16, (entry >> 8) & 7, jnp.concatenate(outs, axis=0)

    def several(start, count):
        parts = [half(start + u) for u in range(count)]
        sums = [jnp.dot(p, table_ref[blocks + b], preferred_element_type=jnp.float32) for _, b, p in parts]
        for (s, _, _), q in zip(parts, sums):
            acc_ref[s, first : first + rows, :] += q

    def four(i, carry):
        several(4 * i, 4)
        return carry

    def two(i, carry):
        several(4 * fours + 2 * i, 2)
        return carry

    fours = (n + 1) >> 2
    lax.fori_loop(0, fours, four, 0)
    lax.fori_loop(0, (jnp.maximum(n - 4 * fours, 0) + 1) >> 1, two, 0)


def ready_tables(lat, lon, later_than):
    blocks = lat.shape[0]

    def kernel(lat_hbm, lon_hbm, _, out_ref, held, sems):
        copies = [
            pltpu.make_async_copy(lat_hbm, held, sems.at[0]),
            pltpu.make_async_copy(lon_hbm, out_ref.at[pl.ds(blocks, blocks)], sems.at[1]),
        ]
        for c in copies:
            c.start()
        copies[0].wait()
        for b in range(blocks):
            out_ref[b] = held[b].T
        copies[1].wait()

    return pl.pallas_call(
        kernel,
        out_shape=jax.ShapeDtypeStruct((2 * blocks,) + lat.shape[1:], lat.dtype),
        in_specs=[HBM] * 3,
        out_specs=VMEM,
        scratch_shapes=[pltpu.VMEM(lat.shape, lat.dtype), pltpu.SemaphoreType.DMA((2,))],
        compiler_params=PARAMS,
        cost_estimate=COST,
    )(in_hbm(lat), in_hbm(lon), later_than)


def phase(sources, tails, sign, offsets, tables, acc, coefs, tiles, slots, levels, fields, size, span=None, flops=1):
    low, high = span or (0, levels)
    block = tiles * fields * size
    per_tile = fields * size
    planes = (high - low) * fields
    fresh = acc is None
    count = len(sources)
    own_tails = tails is None
    flow = coefs is not None
    held_levels = high - low

    def kernel(sign_ref, *refs):
        srcs, refs = refs[:count], refs[count:]
        if own_tails:
            tail_srcs = srcs
        else:
            tail_srcs, refs = refs[:count], refs[count:]
        refs = refs[1 if fresh else 2 :]
        if flow:
            upper_hbm, lower_hbm, table_ref, acc_ref, up_ref, down_ref, upper_ref, lower_ref = refs[:8]
        else:
            table_ref, acc_ref = refs[:2]
        src, tail, meta_v, meta_s, entries, sems = refs[-6:]
        heads = [pltpu.make_async_copy(tail_srcs[g].at[pl.ds(block, META)], tail.at[g], sems.at[g]) for g in range(count)]
        metas = [pltpu.make_async_copy(meta_v.at[g], meta_s.at[g], sems.at[g]) for g in range(count)]
        datas = []
        for g in range(count):
            for l in range(held_levels):
                at = l * block + (META if low == 0 and l > 0 else 0)
                datas.append(pltpu.make_async_copy(srcs[g].at[pl.ds(at, block)], src.at[g, l], sems.at[count + len(datas)]))
        late = []
        if flow:
            late = [
                pltpu.make_async_copy(upper_hbm, upper_ref, sems.at[count + len(datas)]),
                pltpu.make_async_copy(lower_hbm, lower_ref, sems.at[count + len(datas) + 1]),
            ]
        for c in heads + datas + late:
            c.start()
        if fresh:
            acc_ref[...] = jnp.zeros_like(acc_ref)
        for g in range(count):
            heads[g].wait()
            slot_data = tail[g].astype(jnp.float32)
            meta_v[g] = (slot_data[0:1] * 64.0 + slot_data[1:2]).astype(jnp.int32)
            metas[g].start()
        n = 0
        for g in range(count):
            metas[g].wait()
            n = append_slots((REACH - offsets[g] * sign_ref[0]) * tiles, tiles, slots, g, meta_s.at[g], entries, n)
        entries[n] = tiles << 16
        for c in datas:
            c.wait()

        def load(where):
            at = pl.ds(pl.multiple_of(where % tiles * per_tile, per_tile), per_tile)
            rows = [src[where // tiles, l, at, :] for l in range(held_levels)]
            return [r[f * size : (f + 1) * size] for r in rows for f in range(fields)]

        add_slots(n, load, planes, size, low * per_tile, entries, table_ref, acc_ref)
        if not flow:
            return
        for c in late:
            c.wait()
        top = (levels - 1) * per_tile
        for s in range(tiles):
            u = upper_ref[s, levels - 1].astype(jnp.float32)
            d = lower_ref[s, 0].astype(jnp.float32)
            for f in range(fields):
                up_ref[s, f] = (u * acc_ref[s, top + f * size : top + (f + 1) * size]).astype(jnp.bfloat16)
                down_ref[s, f] = (d * acc_ref[s, f * size : (f + 1) * size]).astype(jnp.bfloat16)

    args = [sign, *sources] + ([] if own_tails else list(tails)) + [tables]
    specs = [SMEM] + [HBM] * (len(args) - 2) + [VMEM]
    at = len(args) - 1
    if not fresh:
        args.append(acc)
        specs.append(VMEM)
    out_shape = [
        jax.ShapeDtypeStruct(tables.shape, tables.dtype),
        jax.ShapeDtypeStruct((tiles + 1, levels * per_tile, size), jnp.float32),
    ]
    if flow:
        args += [in_hbm(c) for c in coefs]
        specs += [HBM, HBM]
        out_shape += [jax.ShapeDtypeStruct((tiles, fields, size, size), jnp.bfloat16)] * 2
        out_shape += [jax.ShapeDtypeStruct(c.shape, c.dtype) for c in coefs]
    return pl.pallas_call(
        kernel,
        out_shape=out_shape,
        in_specs=specs,
        out_specs=[VMEM] * len(out_shape),
        scratch_shapes=[
            pltpu.VMEM((count, held_levels, block, size), jnp.bfloat16),
            pltpu.VMEM((count, META, size), jnp.bfloat16),
            pltpu.VMEM((count, 1, size), jnp.int32),
            pltpu.SMEM((count, 1, size), jnp.int32),
            pltpu.SMEM((count * tiles * slots + 2,), jnp.int32),
            pltpu.SemaphoreType.DMA((count * (held_levels + 1) + 2,)),
        ],
        input_output_aliases={at: 0} if fresh else {at: 0, at + 1: 1},
        compiler_params=PARAMS,
        cost_estimate=pl.CostEstimate(flops=flops, transcendentals=0, bytes_accessed=1),
    )(*args)


def couple(out, sums, upper, lower, rim, tiles, levels, fields, size, first, last, flops=1):
    own = last - first

    def kernel(sum_ref, upper_ref, lower_ref, rim_ref, *refs):
        out_ref, buf, sems = refs[-3:]
        copies = []
        for s in range(tiles):
            for l in range(first, last):
                u = upper_ref[s, l].astype(jnp.float32)
                d = lower_ref[s, l].astype(jnp.float32)
                held = 1.0 + u + d
                if l > 0:
                    from_below = upper_ref[s, l - 1].astype(jnp.float32)
                if l < levels - 1:
                    from_above = lower_ref[s, l + 1].astype(jnp.float32)
                for f in range(fields):
                    rows = [slice((m * fields + f) * size, (m * fields + f + 1) * size) for m in range(levels)]
                    edge = rim_ref[s, f].astype(jnp.float32)
                    below = edge if l == 0 else from_below * sum_ref[s, rows[l - 1], :]
                    above = edge if l == levels - 1 else from_above * sum_ref[s, rows[l + 1], :]
                    buf[s, l - first, f] = (held * sum_ref[s, rows[l], :] - below - above).astype(jnp.bfloat16)
            c = pltpu.make_async_copy(buf.at[s], out_ref.at[s, pl.ds(first, own)], sems.at[s])
            c.start()
            copies.append(c)
        for c in copies:
            c.wait()

    args = [sums, upper, lower, rim]
    specs = [VMEM] * 4
    if out is not None:
        args.append(out)
        specs.append(HBM)
    return pl.pallas_call(
        kernel,
        out_shape=jax.ShapeDtypeStruct((tiles, levels, fields, size, size), jnp.bfloat16),
        in_specs=specs,
        out_specs=HBM,
        scratch_shapes=[
            pltpu.VMEM((tiles, own, fields, size, size), jnp.bfloat16),
            pltpu.SemaphoreType.DMA((tiles,)),
        ],
        input_output_aliases={} if out is None else {4: 0},
        compiler_params=PARAMS,
        cost_estimate=pl.CostEstimate(flops=flops, transcendentals=0, bytes_accessed=1),
    )(*args)


def passed_along(x, axis, by):
    length = lax.axis_size(axis)
    pairs = [(i, i + by) for i in range(length) if 0 <= i + by < length]
    return lax.ppermute(x, axis, pairs)


def per_device(
    adj_out, lat_weights, lon_weights, counts, departures, blocks, upper_coef, lower_coef
):
    tile_devices = lax.axis_size("tile")
    own_index = lax.axis_index("tile")
    tiles, slots = departures.shape
    levels, fields, size = adj_out.shape[1], adj_out.shape[2], adj_out.shape[3]
    base_tile = ((own_index - REACH) % tile_devices * tiles).reshape(1)
    packed = pack(adj_out, counts, departures, jnp.swapaxes(blocks, 1, 2), base_tile)

    def permuted(x, even_by, odd_by):
        pairs = [(i, (i + (even_by if i % 2 == 0 else odd_by)) % tile_devices) for i in range(tile_devices)]
        return lax.ppermute(x, "tile", pairs)

    sign = 1 - 2 * (own_index % 2)

    sign = sign.reshape(1).astype(jnp.int32)
    sizes = tiles, slots, levels, fields, size
    x_in = permuted(packed, -2, 2)
    later, tables = lax.optimization_barrier((packed, ready_tables(lat_weights, lon_weights, packed)))
    mate = permuted(later, 1, -1)
    y_in = permuted(later, 2, -2)
    tables, acc = phase((packed,), None, sign, (0,), tables, None, None, *sizes, None, O_FLOPS)
    x_in, acc = lax.optimization_barrier((x_in, acc))
    x_mate = permuted(x_in, 1, -1)
    tables, acc = phase((x_in, mate), None, sign, (2, 1), tables, acc, None, *sizes, None, M_FLOPS)
    x_mate, acc = lax.optimization_barrier((x_mate, acc))
    tables, acc = phase((x_mate,), None, sign, (-1,), tables, acc, None, *sizes, None, XM_FLOPS)
    y_in, acc = lax.optimization_barrier((y_in, acc))
    coefs = upper_coef, lower_coef
    _, acc, up, down, upper, lower = phase((y_in,), None, sign, (-2,), tables, acc, coefs, *sizes, None, L_FLOPS)
    rim_low = passed_along(up, "lev", 1)
    rim_up = passed_along(down, "lev", -1)
    where = tiles, levels, fields, size
    out = couple(None, acc, upper, lower, rim_up, *where, 1, levels, T_FLOPS)
    return couple(out, acc, upper, lower, rim_low, *where, 0, 1)


def solution(mesh):
    placed = (
        P("tile", "lev", None, None, None),
        P(),
        P(),
        P("tile"),
        P("tile", None),
        P("tile", None, None),
        P("tile", "lev", None, None),
        P("tile", "lev", None, None),
    )
    return jax.shard_map(
        per_device,
        mesh=mesh,
        in_specs=placed,
        out_specs=P("tile", "lev", None, None, None),
        check_vma=False,
    )
```

```python
import jax
import jax.numpy as jnp
from jax import lax
from jax.experimental import pallas as pl
from jax.experimental.pallas import tpu as pltpu
from jax.sharding import PartitionSpec as P

REACH = 2
DEAD = 64
META = 16
O_FLOPS = 1 << 0
M_FLOPS = 1 << 36
XM_FLOPS = 1 << 0
L_FLOPS = 1 << 0
T_FLOPS = 1 << 36
VMEM = pl.BlockSpec(memory_space=pltpu.VMEM)
SMEM = pl.BlockSpec(memory_space=pltpu.SMEM)
HBM = pl.BlockSpec(memory_space=pltpu.HBM)
COST = pl.CostEstimate(flops=1, transcendentals=0, bytes_accessed=1)
PARAMS = pltpu.CompilerParams(vmem_limit_bytes=6 << 20)


def in_hbm(x):
    return pltpu.with_memory_space_constraint(x, pltpu.HBM)


def pack(adj_out, counts, departures, blocks, base):
    tiles, levels, fields, size, _ = adj_out.shape
    rows = fields * size
    slots = departures.shape[1]
    wrap = lax.axis_size("tile") * tiles
    flat = adj_out.reshape(tiles, levels, rows, size)

    def kernel(base_ref, counts_hbm, dep_hbm, blk_hbm, flat_hbm, out_ref, counts_ref, dep, blk, meta, sems):
        copies = [
            pltpu.make_async_copy(counts_hbm, counts_ref, sems.at[0]),
            pltpu.make_async_copy(dep_hbm, dep, sems.at[1]),
            pltpu.make_async_copy(blk_hbm, blk, sems.at[2]),
        ]
        for l in range(levels):
            for t in range(tiles):
                at = (l * tiles + t) * rows + (META if l else 0)
                copies.append(
                    pltpu.make_async_copy(flat_hbm.at[t, l], out_ref.at[pl.ds(at, rows)], sems.at[3 + l * tiles + t])
                )
        for c in copies:
            c.start()
        meta[...] = jnp.zeros_like(meta)
        for c in copies[:3]:
            c.wait()
        w = dep[...] - base_ref[0]
        w = jnp.where(w < 0, w + wrap, w)
        k = lax.broadcasted_iota(jnp.int32, (1, slots), 1)
        for t in range(tiles):
            at = slice(t * slots, (t + 1) * slots)
            meta[0:1, at] = jnp.where(k < counts_ref[t], w[t : t + 1], DEAD).astype(jnp.float32)
            meta[1:2, at] = (blk[t, 0:1] * 8 + blk[t, 1:2]).astype(jnp.float32)
        out_ref[tiles * rows : tiles * rows + META, :] = meta[...].astype(jnp.bfloat16)
        for c in copies[3:]:
            c.wait()

    return pl.pallas_call(
        kernel,
        out_shape=jax.ShapeDtypeStruct((tiles * levels * rows + META, size), adj_out.dtype),
        in_specs=[SMEM, HBM, HBM, HBM, HBM],
        out_specs=VMEM,
        scratch_shapes=[
            pltpu.SMEM((tiles,), jnp.int32),
            pltpu.VMEM((tiles, slots), jnp.int32),
            pltpu.VMEM((tiles, 2, slots), jnp.int32),
            pltpu.VMEM((META, size), jnp.float32),
            pltpu.SemaphoreType.DMA((3 + tiles * levels,)),
        ],
        compiler_params=PARAMS,
        cost_estimate=COST,
    )(base, in_hbm(counts), in_hbm(departures), in_hbm(blocks), in_hbm(flat))


def append_slots(shift, tiles, slots, where, meta_s, entries, n):
    for t in range(tiles):
        for k in range(slots):
            code = meta_s[0, t * slots + k]
            s = (code >> 6) - shift
            entries[n] = (s << 16) | ((code & 63) << 8) | (where * tiles + t)
            n = n + jnp.logical_and(s >= 0, s < tiles).astype(jnp.int32)
    return n


def add_slots(n, load, planes, size, first, entries, table_ref, acc_ref):
    blocks = table_ref.shape[0] // 2
    rows = planes * size

    def half(i):
        entry = entries[i]
        a = load(entry & 255)
        lat_t = table_ref[(entry >> 11) & 7]
        outs = []
        for j in range(0, planes, 2):
            if j + 1 == planes:
                wide = a[j]
            else:
                wide = jnp.concatenate([a[j], a[j + 1]], axis=1)
            p = jnp.dot(lat_t, wide, preferred_element_type=jnp.float32).astype(jnp.bfloat16)
            outs += [p] if j + 1 == planes else [p[:, :size], p[:, size:]]
        return entry >> 16, (entry >> 8) & 7, jnp.concatenate(outs, axis=0)

    def several(start, count):
        parts = [half(start + u) for u in range(count)]
        sums = [jnp.dot(p, table_ref[blocks + b], preferred_element_type=jnp.float32) for _, b, p in parts]
        for (s, _, _), q in zip(parts, sums):
            acc_ref[s, first : first + rows, :] += q

    def four(i, carry):
        several(4 * i, 4)
        return carry

    def two(i, carry):
        several(4 * fours + 2 * i, 2)
        return carry

    fours = (n + 1) >> 2
    lax.fori_loop(0, fours, four, 0)
    lax.fori_loop(0, (jnp.maximum(n - 4 * fours, 0) + 1) >> 1, two, 0)


def ready_tables(lat, lon, later_than):
    blocks = lat.shape[0]

    def kernel(lat_hbm, lon_hbm, _, out_ref, held, sems):
        copies = [
            pltpu.make_async_copy(lat_hbm, held, sems.at[0]),
            pltpu.make_async_copy(lon_hbm, out_ref.at[pl.ds(blocks, blocks)], sems.at[1]),
        ]
        for c in copies:
            c.start()
        copies[0].wait()
        for b in range(blocks):
            out_ref[b] = held[b].T
        copies[1].wait()

    return pl.pallas_call(
        kernel,
        out_shape=jax.ShapeDtypeStruct((2 * blocks,) + lat.shape[1:], lat.dtype),
        in_specs=[HBM] * 3,
        out_specs=VMEM,
        scratch_shapes=[pltpu.VMEM(lat.shape, lat.dtype), pltpu.SemaphoreType.DMA((2,))],
        compiler_params=PARAMS,
        cost_estimate=COST,
    )(in_hbm(lat), in_hbm(lon), later_than)


def phase(sources, sign, offsets, tables, acc, coefs, tiles, slots, levels, fields, size, flops=1):
    block = tiles * fields * size
    per_tile = fields * size
    planes = levels * fields
    fresh = acc is None
    count = len(sources)
    flow = coefs is not None

    def kernel(sign_ref, *refs):
        srcs, refs = refs[:count], refs[count:]
        refs = refs[1 if fresh else 2 :]
        if flow:
            upper_hbm, lower_hbm, table_ref, acc_ref, up_ref, down_ref, upper_ref, lower_ref = refs[:8]
        else:
            table_ref, acc_ref = refs[:2]
        meta_v, meta_s, entries, sems = refs[-4:]
        metas = [pltpu.make_async_copy(meta_v.at[g], meta_s.at[g], sems.at[g]) for g in range(count)]
        late = []
        if flow:
            late = [
                pltpu.make_async_copy(upper_hbm, upper_ref, sems.at[count]),
                pltpu.make_async_copy(lower_hbm, lower_ref, sems.at[count + 1]),
            ]
        for c in late:
            c.start()
        for g in range(count):
            slot_data = srcs[g][block : block + META, :].astype(jnp.float32)
            meta_v[g] = (slot_data[0:1] * 64.0 + slot_data[1:2]).astype(jnp.int32)
            metas[g].start()
        if fresh:
            acc_ref[...] = jnp.zeros_like(acc_ref)
        for g in range(count):
            metas[g].wait()
            n = append_slots((REACH - offsets[g] * sign_ref[0]) * tiles, tiles, slots, 0, meta_s.at[g], entries, 0)
            entries[n] = tiles << 16

            def load(t, ref=srcs[g]):
                rows = []
                for l in range(levels):
                    at = pl.multiple_of(t * per_tile, per_tile) + (l * block + META if l else 0)
                    rows.append(ref[pl.ds(pl.multiple_of(at, 16), per_tile), :])
                return [r[f * size : (f + 1) * size] for r in rows for f in range(fields)]

            add_slots(n, load, planes, size, 0, entries, table_ref, acc_ref)
        if not flow:
            return
        for c in late:
            c.wait()
        top = (levels - 1) * per_tile
        for s in range(tiles):
            u = upper_ref[s, levels - 1].astype(jnp.float32)
            d = lower_ref[s, 0].astype(jnp.float32)
            for f in range(fields):
                up_ref[s, f] = (u * acc_ref[s, top + f * size : top + (f + 1) * size]).astype(jnp.bfloat16)
                down_ref[s, f] = (d * acc_ref[s, f * size : (f + 1) * size]).astype(jnp.bfloat16)

    args = [sign, *sources, tables]
    specs = [SMEM] + [VMEM] * (count + 1)
    at = len(args) - 1
    if not fresh:
        args.append(acc)
        specs.append(VMEM)
    out_shape = [
        jax.ShapeDtypeStruct(tables.shape, tables.dtype),
        jax.ShapeDtypeStruct((tiles + 1, levels * per_tile, size), jnp.float32),
    ]
    if flow:
        args += [in_hbm(c) for c in coefs]
        specs += [HBM, HBM]
        out_shape += [jax.ShapeDtypeStruct((tiles, fields, size, size), jnp.bfloat16)] * 2
        out_shape += [jax.ShapeDtypeStruct(c.shape, c.dtype) for c in coefs]
    return pl.pallas_call(
        kernel,
        out_shape=out_shape,
        in_specs=specs,
        out_specs=[VMEM] * len(out_shape),
        scratch_shapes=[
            pltpu.VMEM((count, 1, size), jnp.int32),
            pltpu.SMEM((count, 1, size), jnp.int32),
            pltpu.SMEM((tiles * slots + 2,), jnp.int32),
            pltpu.SemaphoreType.DMA((count + 2,)),
        ],
        input_output_aliases={at: 0} if fresh else {at: 0, at + 1: 1},
        compiler_params=PARAMS,
        cost_estimate=pl.CostEstimate(flops=flops, transcendentals=0, bytes_accessed=1),
    )(*args)


def couple(out, sums, upper, lower, rim, tiles, levels, fields, size, first, last, flops=1):
    own = last - first

    def kernel(sum_ref, upper_ref, lower_ref, rim_ref, *refs):
        out_ref, buf, sems = refs[-3:]
        copies = []
        for s in range(tiles):
            for l in range(first, last):
                u = upper_ref[s, l].astype(jnp.float32)
                d = lower_ref[s, l].astype(jnp.float32)
                held = 1.0 + u + d
                if l > 0:
                    from_below = upper_ref[s, l - 1].astype(jnp.float32)
                if l < levels - 1:
                    from_above = lower_ref[s, l + 1].astype(jnp.float32)
                for f in range(fields):
                    rows = [slice((m * fields + f) * size, (m * fields + f + 1) * size) for m in range(levels)]
                    edge = rim_ref[s, f].astype(jnp.float32)
                    below = edge if l == 0 else from_below * sum_ref[s, rows[l - 1], :]
                    above = edge if l == levels - 1 else from_above * sum_ref[s, rows[l + 1], :]
                    buf[s, l - first, f] = (held * sum_ref[s, rows[l], :] - below - above).astype(jnp.bfloat16)
            c = pltpu.make_async_copy(buf.at[s], out_ref.at[s, pl.ds(first, own)], sems.at[s])
            c.start()
            copies.append(c)
        for c in copies:
            c.wait()

    args = [sums, upper, lower, rim]
    specs = [VMEM] * 4
    if out is not None:
        args.append(out)
        specs.append(HBM)
    return pl.pallas_call(
        kernel,
        out_shape=jax.ShapeDtypeStruct((tiles, levels, fields, size, size), jnp.bfloat16),
        in_specs=specs,
        out_specs=HBM,
        scratch_shapes=[
            pltpu.VMEM((tiles, own, fields, size, size), jnp.bfloat16),
            pltpu.SemaphoreType.DMA((tiles,)),
        ],
        input_output_aliases={} if out is None else {4: 0},
        compiler_params=PARAMS,
        cost_estimate=pl.CostEstimate(flops=flops, transcendentals=0, bytes_accessed=1),
    )(*args)


def passed_along(x, axis, by):
    length = lax.axis_size(axis)
    pairs = [(i, i + by) for i in range(length) if 0 <= i + by < length]
    return lax.ppermute(x, axis, pairs)


def per_device(
    adj_out, lat_weights, lon_weights, counts, departures, blocks, upper_coef, lower_coef
):
    tile_devices = lax.axis_size("tile")
    own_index = lax.axis_index("tile")
    tiles, slots = departures.shape
    levels, fields, size = adj_out.shape[1], adj_out.shape[2], adj_out.shape[3]
    base_tile = ((own_index - REACH) % tile_devices * tiles).reshape(1)
    packed = pack(adj_out, counts, departures, jnp.swapaxes(blocks, 1, 2), base_tile)

    def permuted(x, even_by, odd_by):
        pairs = [(i, (i + (even_by if i % 2 == 0 else odd_by)) % tile_devices) for i in range(tile_devices)]
        return lax.ppermute(x, "tile", pairs)

    sign = 1 - 2 * (own_index % 2)

    sign = sign.reshape(1).astype(jnp.int32)
    sizes = tiles, slots, levels, fields, size
    x_in = permuted(packed, -2, 2)
    mate, tables = lax.optimization_barrier((packed, ready_tables(lat_weights, lon_weights, packed)))
    mate = permuted(mate, 1, -1)
    tables, acc = phase((packed,), sign, (0,), tables, None, None, *sizes, O_FLOPS)
    y_in, acc = lax.optimization_barrier((packed, acc))
    y_in = permuted(y_in, 2, -2)
    x_in, acc = lax.optimization_barrier((x_in, acc))
    x_mate = permuted(x_in, 1, -1)
    tables, acc = phase((x_in, mate), sign, (2, 1), tables, acc, None, *sizes, M_FLOPS)
    x_mate, acc = lax.optimization_barrier((x_mate, acc))
    tables, acc = phase((x_mate,), sign, (-1,), tables, acc, None, *sizes, XM_FLOPS)
    y_in, acc = lax.optimization_barrier((y_in, acc))
    coefs = upper_coef, lower_coef
    _, acc, up, down, upper, lower = phase((y_in,), sign, (-2,), tables, acc, coefs, *sizes, L_FLOPS)
    rim_low = passed_along(up, "lev", 1)
    rim_up = passed_along(down, "lev", -1)
    where = tiles, levels, fields, size
    out = couple(None, acc, upper, lower, rim_up, *where, 1, levels, T_FLOPS)
    return couple(out, acc, upper, lower, rim_low, *where, 0, 1)


def solution(mesh):
    placed = (
        P("tile", "lev", None, None, None),
        P(),
        P(),
        P("tile"),
        P("tile", None),
        P("tile", None, None),
        P("tile", "lev", None, None),
        P("tile", "lev", None, None),
    )
    return jax.shard_map(
        per_device,
        mesh=mesh,
        in_specs=placed,
        out_specs=P("tile", "lev", None, None, None),
        check_vma=False,
    )
```

```python
import jax
import jax.numpy as jnp
from jax import lax
from jax.experimental import pallas as pl
from jax.experimental.pallas import tpu as pltpu
from jax.sharding import PartitionSpec as P

REACH = 2
DEAD = 64
META = 16
O_FLOPS = 1 << 0
M_FLOPS = 1 << 36
XM_FLOPS = 1 << 0
L_FLOPS = 1 << 0
T_FLOPS = 1 << 36
VMEM = pl.BlockSpec(memory_space=pltpu.VMEM)
SMEM = pl.BlockSpec(memory_space=pltpu.SMEM)
HBM = pl.BlockSpec(memory_space=pltpu.HBM)
COST = pl.CostEstimate(flops=1, transcendentals=0, bytes_accessed=1)
PARAMS = pltpu.CompilerParams(vmem_limit_bytes=6 << 20)


def in_hbm(x):
    return pltpu.with_memory_space_constraint(x, pltpu.HBM)


def pack(adj_out, counts, departures, blocks, base):
    tiles, levels, fields, size, _ = adj_out.shape
    rows = fields * size
    slots = departures.shape[1]
    wrap = lax.axis_size("tile") * tiles
    flat = adj_out.reshape(tiles, levels, rows, size)

    def kernel(base_ref, counts_hbm, dep_hbm, blk_hbm, flat_hbm, out_ref, counts_ref, dep, blk, meta, sems):
        copies = [
            pltpu.make_async_copy(counts_hbm, counts_ref, sems.at[0]),
            pltpu.make_async_copy(dep_hbm, dep, sems.at[1]),
            pltpu.make_async_copy(blk_hbm, blk, sems.at[2]),
        ]
        for l in range(levels):
            for t in range(tiles):
                at = (l * tiles + t) * rows + (META if l else 0)
                copies.append(
                    pltpu.make_async_copy(flat_hbm.at[t, l], out_ref.at[pl.ds(at, rows)], sems.at[3 + l * tiles + t])
                )
        for c in copies:
            c.start()
        meta[...] = jnp.zeros_like(meta)
        for c in copies[:3]:
            c.wait()
        w = dep[...] - base_ref[0]
        w = jnp.where(w < 0, w + wrap, w)
        k = lax.broadcasted_iota(jnp.int32, (1, slots), 1)
        for t in range(tiles):
            at = slice(t * slots, (t + 1) * slots)
            meta[0:1, at] = jnp.where(k < counts_ref[t], w[t : t + 1], DEAD).astype(jnp.float32)
            meta[1:2, at] = (blk[t, 0:1] * 8 + blk[t, 1:2]).astype(jnp.float32)
        out_ref[tiles * rows : tiles * rows + META, :] = meta[...].astype(jnp.bfloat16)
        for c in copies[3:]:
            c.wait()

    return pl.pallas_call(
        kernel,
        out_shape=jax.ShapeDtypeStruct((tiles * levels * rows + META, size), adj_out.dtype),
        in_specs=[SMEM, HBM, HBM, HBM, HBM],
        out_specs=VMEM,
        scratch_shapes=[
            pltpu.SMEM((tiles,), jnp.int32),
            pltpu.VMEM((tiles, slots), jnp.int32),
            pltpu.VMEM((tiles, 2, slots), jnp.int32),
            pltpu.VMEM((META, size), jnp.float32),
            pltpu.SemaphoreType.DMA((3 + tiles * levels,)),
        ],
        compiler_params=PARAMS,
        cost_estimate=COST,
    )(base, in_hbm(counts), in_hbm(departures), in_hbm(blocks), in_hbm(flat))


def append_slots(shift, tiles, slots, where, meta_s, entries, n):
    for t in range(tiles):
        for k in range(slots):
            code = meta_s[0, t * slots + k]
            s = (code >> 6) - shift
            entries[n] = (s << 16) | ((code & 63) << 8) | (where * tiles + t)
            n = n + jnp.logical_and(s >= 0, s < tiles).astype(jnp.int32)
    return n


def add_slots(n, load, planes, size, first, entries, table_ref, acc_ref):
    blocks = table_ref.shape[0] // 2
    rows = planes * size

    def half(i):
        entry = entries[i]
        a = load(entry & 255)
        lat_t = table_ref[(entry >> 11) & 7]
        outs = []
        for j in range(0, planes, 2):
            if j + 1 == planes:
                wide = a[j]
            else:
                wide = jnp.concatenate([a[j], a[j + 1]], axis=1)
            p = jnp.dot(lat_t, wide, preferred_element_type=jnp.float32).astype(jnp.bfloat16)
            outs += [p] if j + 1 == planes else [p[:, :size], p[:, size:]]
        return entry >> 16, (entry >> 8) & 7, jnp.concatenate(outs, axis=0)

    def several(start, count):
        parts = [half(start + u) for u in range(count)]
        sums = [jnp.dot(p, table_ref[blocks + b], preferred_element_type=jnp.float32) for _, b, p in parts]
        for (s, _, _), q in zip(parts, sums):
            acc_ref[s, first : first + rows, :] += q

    def four(i, carry):
        several(4 * i, 4)
        return carry

    def two(i, carry):
        several(4 * fours + 2 * i, 2)
        return carry

    fours = (n + 1) >> 2
    lax.fori_loop(0, fours, four, 0)
    lax.fori_loop(0, (jnp.maximum(n - 4 * fours, 0) + 1) >> 1, two, 0)


def phase(sources, sign, offsets, tables, acc, coefs, tiles, slots, levels, fields, size, flops=1):
    block = tiles * fields * size
    per_tile = fields * size
    planes = levels * fields
    fresh = acc is None
    count = len(sources)
    flow = coefs is not None

    def kernel(sign_ref, *refs):
        srcs, refs = refs[:count], refs[count:]
        lat_hbm, lon_hbm = refs[:2]
        refs = refs[2:]
        if flow:
            upper_hbm, lower_hbm, table_ref, acc_ref, up_ref, down_ref, upper_ref, lower_ref = refs[:8]
        else:
            table_ref, acc_ref = refs[:2]
        meta_v, meta_s, entries, sems = refs[-5:-1] if fresh else refs[-4:]
        held = refs[-1]
        metas = [pltpu.make_async_copy(meta_v.at[g], meta_s.at[g], sems.at[g]) for g in range(count)]
        late = []
        if flow:
            late = [
                pltpu.make_async_copy(upper_hbm, upper_ref, sems.at[count]),
                pltpu.make_async_copy(lower_hbm, lower_ref, sems.at[count + 1]),
            ]
        if fresh:
            late = [
                pltpu.make_async_copy(lat_hbm, held, sems.at[count]),
                pltpu.make_async_copy(lon_hbm, table_ref.at[pl.ds(lon_hbm.shape[0], lon_hbm.shape[0])], sems.at[count + 1]),
            ]
        for c in late:
            c.start()
        for g in range(count):
            slot_data = srcs[g][block : block + META, :].astype(jnp.float32)
            meta_v[g] = (slot_data[0:1] * 64.0 + slot_data[1:2]).astype(jnp.int32)
            metas[g].start()
        if fresh:
            acc_ref[...] = jnp.zeros_like(acc_ref)
        for g in range(count):
            metas[g].wait()
            n = append_slots((REACH - offsets[g] * sign_ref[0]) * tiles, tiles, slots, 0, meta_s.at[g], entries, 0)
            entries[n] = tiles << 16
            if fresh and g == 0:
                for c in late:
                    c.wait()
                for b in range(lat_hbm.shape[0]):
                    table_ref[b] = held[b].T

            def load(t, ref=srcs[g]):
                rows = []
                for l in range(levels):
                    at = pl.multiple_of(t * per_tile, per_tile) + (l * block + META if l else 0)
                    rows.append(ref[pl.ds(pl.multiple_of(at, 16), per_tile), :])
                return [r[f * size : (f + 1) * size] for r in rows for f in range(fields)]

            add_slots(n, load, planes, size, 0, entries, table_ref, acc_ref)
        if not flow:
            return
        for c in late:
            c.wait()
        top = (levels - 1) * per_tile
        for s in range(tiles):
            u = upper_ref[s, levels - 1].astype(jnp.float32)
            d = lower_ref[s, 0].astype(jnp.float32)
            for f in range(fields):
                up_ref[s, f] = (u * acc_ref[s, top + f * size : top + (f + 1) * size]).astype(jnp.bfloat16)
                down_ref[s, f] = (d * acc_ref[s, f * size : (f + 1) * size]).astype(jnp.bfloat16)

    if fresh:
        args = [sign, *sources] + [in_hbm(t) for t in tables]
        specs = [SMEM] + [VMEM] * count + [HBM] * 2
        table_shape = (tables[0].shape[0] + tables[1].shape[0],) + tables[0].shape[1:]
    else:
        args = [sign, *sources, tables]
        specs = [SMEM] + [VMEM] * (count + 1)
        table_shape = tables.shape
    at = len(args) - 1
    if not fresh:
        args.append(acc)
        specs.append(VMEM)
    out_shape = [
        jax.ShapeDtypeStruct(table_shape, sources[0].dtype),
        jax.ShapeDtypeStruct((tiles + 1, levels * per_tile, size), jnp.float32),
    ]
    if flow:
        args += [in_hbm(c) for c in coefs]
        specs += [HBM, HBM]
        out_shape += [jax.ShapeDtypeStruct((tiles, fields, size, size), jnp.bfloat16)] * 2
        out_shape += [jax.ShapeDtypeStruct(c.shape, c.dtype) for c in coefs]
    return pl.pallas_call(
        kernel,
        out_shape=out_shape,
        in_specs=specs,
        out_specs=[VMEM] * len(out_shape),
        scratch_shapes=[
            pltpu.VMEM((count, 1, size), jnp.int32),
            pltpu.SMEM((count, 1, size), jnp.int32),
            pltpu.SMEM((tiles * slots + 2,), jnp.int32),
            pltpu.SemaphoreType.DMA((count + 2,)),
        ]
        + ([pltpu.VMEM(tables[0].shape, tables[0].dtype)] if fresh else []),
        input_output_aliases={} if fresh else {at: 0, at + 1: 1},
        compiler_params=PARAMS,
        cost_estimate=pl.CostEstimate(flops=flops, transcendentals=0, bytes_accessed=1),
    )(*args)


def couple(out, sums, upper, lower, rim, tiles, levels, fields, size, first, last, flops=1):
    own = last - first

    def kernel(sum_ref, upper_ref, lower_ref, rim_ref, *refs):
        out_ref, buf, sems = refs[-3:]
        copies = []
        for s in range(tiles):
            for l in range(first, last):
                u = upper_ref[s, l].astype(jnp.float32)
                d = lower_ref[s, l].astype(jnp.float32)
                held = 1.0 + u + d
                if l > 0:
                    from_below = upper_ref[s, l - 1].astype(jnp.float32)
                if l < levels - 1:
                    from_above = lower_ref[s, l + 1].astype(jnp.float32)
                for f in range(fields):
                    rows = [slice((m * fields + f) * size, (m * fields + f + 1) * size) for m in range(levels)]
                    edge = rim_ref[s, f].astype(jnp.float32)
                    below = edge if l == 0 else from_below * sum_ref[s, rows[l - 1], :]
                    above = edge if l == levels - 1 else from_above * sum_ref[s, rows[l + 1], :]
                    buf[s, l - first, f] = (held * sum_ref[s, rows[l], :] - below - above).astype(jnp.bfloat16)
            c = pltpu.make_async_copy(buf.at[s], out_ref.at[s, pl.ds(first, own)], sems.at[s])
            c.start()
            copies.append(c)
        for c in copies:
            c.wait()

    args = [sums, upper, lower, rim]
    specs = [VMEM] * 4
    if out is not None:
        args.append(out)
        specs.append(HBM)
    return pl.pallas_call(
        kernel,
        out_shape=jax.ShapeDtypeStruct((tiles, levels, fields, size, size), jnp.bfloat16),
        in_specs=specs,
        out_specs=HBM,
        scratch_shapes=[
            pltpu.VMEM((tiles, own, fields, size, size), jnp.bfloat16),
            pltpu.SemaphoreType.DMA((tiles,)),
        ],
        input_output_aliases={} if out is None else {4: 0},
        compiler_params=PARAMS,
        cost_estimate=pl.CostEstimate(flops=flops, transcendentals=0, bytes_accessed=1),
    )(*args)


def passed_along(x, axis, by):
    length = lax.axis_size(axis)
    pairs = [(i, i + by) for i in range(length) if 0 <= i + by < length]
    return lax.ppermute(x, axis, pairs)


def per_device(
    adj_out, lat_weights, lon_weights, counts, departures, blocks, upper_coef, lower_coef
):
    tile_devices = lax.axis_size("tile")
    own_index = lax.axis_index("tile")
    tiles, slots = departures.shape
    levels, fields, size = adj_out.shape[1], adj_out.shape[2], adj_out.shape[3]
    base_tile = ((own_index - REACH) % tile_devices * tiles).reshape(1)
    packed = pack(adj_out, counts, departures, jnp.swapaxes(blocks, 1, 2), base_tile)

    def permuted(x, even_by, odd_by):
        pairs = [(i, (i + (even_by if i % 2 == 0 else odd_by)) % tile_devices) for i in range(tile_devices)]
        return lax.ppermute(x, "tile", pairs)

    sign = 1 - 2 * (own_index % 2)

    sign = sign.reshape(1).astype(jnp.int32)
    sizes = tiles, slots, levels, fields, size
    x_in = permuted(packed, -2, 2)
    tables, acc = phase((packed,), sign, (0,), (lat_weights, lon_weights), None, None, *sizes, O_FLOPS)
    later, acc = lax.optimization_barrier((packed, acc))
    mate = permuted(later, 1, -1)
    y_in = permuted(later, 2, -2)
    x_in, acc = lax.optimization_barrier((x_in, acc))
    x_mate = permuted(x_in, 1, -1)
    tables, acc = phase((x_in, mate), sign, (2, 1), tables, acc, None, *sizes, M_FLOPS)
    x_mate, acc = lax.optimization_barrier((x_mate, acc))
    tables, acc = phase((x_mate,), sign, (-1,), tables, acc, None, *sizes, XM_FLOPS)
    y_in, acc = lax.optimization_barrier((y_in, acc))
    coefs = upper_coef, lower_coef
    _, acc, up, down, upper, lower = phase((y_in,), sign, (-2,), tables, acc, coefs, *sizes, L_FLOPS)
    rim_low = passed_along(up, "lev", 1)
    rim_up = passed_along(down, "lev", -1)
    where = tiles, levels, fields, size
    out = couple(None, acc, upper, lower, rim_up, *where, 1, levels, T_FLOPS)
    return couple(out, acc, upper, lower, rim_low, *where, 0, 1)


def solution(mesh):
    placed = (
        P("tile", "lev", None, None, None),
        P(),
        P(),
        P("tile"),
        P("tile", None),
        P("tile", None, None),
        P("tile", "lev", None, None),
        P("tile", "lev", None, None),
    )
    return jax.shard_map(
        per_device,
        mesh=mesh,
        in_specs=placed,
        out_specs=P("tile", "lev", None, None, None),
        check_vma=False,
    )
```
